32 devices in a mesh: rows: 8 (over y, x, core), snap: 4 (over z).
Axes of the slice: x: 2, y: 2, z: 4, core: 2. Of those that a mesh axis runs over, the one named last changes fastest.
Arguments:
- direct: bfloat16 [65536, 1024], P('rows', 'snap'), may hold values from -6 to 6
- adjoint: bfloat16 [65536, 1024], P('rows', 'snap'), may hold values from -6 to 6
- right_vectors: bfloat16 [1024, 256], replicated, may hold values from -0.1875 to 0.1875
- left_vectors: bfloat16 [1024, 256], replicated, may hold values from -0.1875 to 0.1875
- singular: float32 [256], replicated, may hold values from 0.25 to 4
Outputs:
- gram: float32 [1024, 1024], P('snap', 'rows')
- balancing: bfloat16 [65536, 256], P('rows', 'snap')
- adjoint_modes: bfloat16 [65536, 256], P('rows', 'snap')
The draws below stay inside these ranges and needn't reach their ends.
All inputs are finite; a program needn't handle non-finite values.
Results may differ from the reference program's by a relative error of at most 0.0045.
Values may be sent and summed in bfloat16 or wider, within the bound.
A program may use at most 128 MiB of HBM per device.

```python
import math
import jax
import jax.numpy as jnp
from jax import lax

M = 1024
R = 256
NROWS = 65536


def strengthened(array, key, source, target, blocks, factor):
    def block_of(position):
        return (jnp.arange(array.shape[position]) // (array.shape[position] // blocks)).reshape((-1,) + (1,) * (array.ndim - 1 - position))

    first = jax.random.permutation(key, blocks)[block_of(target)]
    other_side = (block_of(target) + blocks // 2) % blocks
    return jnp.where((block_of(source) == first) | (block_of(source) == other_side), factor * array, array)


def shard_levels(stream_key, dims, pieces, low, high):
    level = 1.0
    for axis_at, shards_of in pieces:
        steps = jax.random.uniform(jax.random.fold_in(jax.random.fold_in(stream_key, 6), axis_at), (shards_of,), jnp.float32, low / len(pieces), high / len(pieces))
        level = level * jnp.repeat(jnp.exp(steps), dims[axis_at] // shards_of).reshape((-1,) + (1,) * (len(dims) - 1 - axis_at))
    return level


def scatter_about(key, shape, spread, most, pieces=(), dtype=jnp.bfloat16):
    values = spread * jax.random.normal(key, shape, jnp.float32)
    if pieces:
        values = values * shard_levels(key, shape, pieces, -0.22, 0.18)
    return jnp.clip(values, -most, most).astype(dtype)


def noise_with(own_key, extent, spread, reach, shards, heavy, kind=jnp.bfloat16):
    array = spread * jax.random.normal(own_key, extent, jnp.float32)
    if shards:
        array = array * shard_levels(own_key, extent, shards, -0.22, 0.18)
    return jnp.clip(strengthened(array, jax.random.fold_in(own_key, 3), *heavy), -reach, reach).astype(kind)


def setup_inputs(seed: int = 0) -> dict:
    seeds = jax.random.split(jax.random.key(seed), 6)
    direct = noise_with(seeds[0], (NROWS, M), 1.0, 6.0, ((0, 8), (1, 4)), (0, 1, 8, 2.0))
    adjoint = scatter_about(seeds[1], (NROWS, M), 1.0, 6.0, ((0, 8), (1, 4)))
    right_vectors = scatter_about(seeds[2], (M, R), M ** -0.5, 0.1875)
    left_vectors = scatter_about(seeds[3], (M, R), M ** -0.5, 0.1875)
    singular = jnp.clip(jnp.exp(jax.random.uniform(seeds[4], (R,), jnp.float32, math.log(0.25), math.log(4.0))), 0.25, 4.0)
    return {"direct": direct, "adjoint": adjoint, "right_vectors": right_vectors, "left_vectors": left_vectors, "singular": singular}


def reference(direct, adjoint, right_vectors, left_vectors, singular):
    nrows = direct.shape[0]
    cross = lax.dot_general(adjoint, direct, (((0,), (0,)), ((), ())), preferred_element_type=jnp.float32)
    gram = cross / jnp.sqrt(jnp.float32(nrows))
    weights = lax.rsqrt(singular.astype(jnp.float32))
    balancing = (jnp.dot(direct, right_vectors, preferred_element_type=jnp.float32) * weights).astype(jnp.bfloat16)
    adjoint_modes = (jnp.dot(adjoint, left_vectors, preferred_element_type=jnp.float32) * weights).astype(jnp.bfloat16)
    return (gram, balancing, adjoint_modes)
```

```python
import jax
import jax.numpy as jnp
from jax import lax
from jax.sharding import PartitionSpec as P

CHUNKS = 2


def shifted(block, level):
    count = lax.axis_size("snap")
    return lax.ppermute(block, "snap", [(k, k ^ (1 << level)) for k in range(count)])


def swapped_by(blocks, index):
    level = 0
    while (1 << level) < len(blocks):
        odd = (index >> level) % 2 == 1
        blocks = [jnp.where(odd, blocks[k ^ (1 << level)], blocks[k]) for k in range(len(blocks))]
        level += 1
    return blocks


def gram_dot(y, x):
    return lax.dot_general(y, x, (((0,), (0,)), ((), ())), preferred_element_type=jnp.float32)


def mode_dot(block, vectors):
    return lax.dot_general(vectors, block, (((0,), (1,)), ((), ())), preferred_element_type=jnp.float32)


def on_device(direct, adjoint, right_vectors, left_vectors, singular):
    local_rows, block_cols = direct.shape
    modes_all = right_vectors.shape[1]
    nsnap = lax.axis_size("snap")
    nrow_devices = lax.axis_size("rows")
    mode_cols = modes_all // nsnap
    me = lax.axis_index("snap")
    my_row = lax.axis_index("rows")
    nrows = local_rows * nrow_devices
    nbits = nsnap.bit_length() - 1
    weights = lax.rsqrt(lax.dynamic_slice_in_dim(singular, me * mode_cols, mode_cols, 0))[:, None]

    def vectors_block(vectors, row_block, mode_block):
        return lax.dynamic_slice(
            vectors, (row_block * block_cols, mode_block * mode_cols), (block_cols, mode_cols)
        )

    step = local_rows // CHUNKS
    y_own = [adjoint[c * step : (c + 1) * step] for c in range(CHUNKS)]
    x_all = [[direct[c * step : (c + 1) * step]] for c in range(CHUNKS)]
    y_oth = []
    for c in range(CHUNKS):
        y_oth.append(shifted(y_own[c], 0))
        for level in range(1, nbits):
            x_all[c] = x_all[c] + [shifted(b, level) for b in x_all[c]]

    terms = []
    parts = []
    tiles = {}
    for c in range(CHUNKS):
        terms.append(
            [
                mode_dot(y_own[c], vectors_block(left_vectors, me, me ^ (2 * e)))
                + mode_dot(y_oth[c], vectors_block(left_vectors, me ^ 1, me ^ (2 * e)))
                for e in range(nsnap // 2)
            ]
        )
        parts.append(
            [
                sum(
                    mode_dot(x_all[c][e], vectors_block(right_vectors, me ^ (2 * e), me ^ a))
                    for e in range(nsnap // 2)
                )
                for a in range(2)
            ]
        )
        for e in range(nsnap // 2):
            for a, y in enumerate((y_own[c], y_oth[c])):
                tile = gram_dot(y, x_all[c][e])
                tiles[e, a] = tile if c == 0 else tiles[e, a] + tile

    last = x_all[CHUNKS - 1][nsnap // 2 - 1]
    balancing = []
    adjoint_modes = []
    for c in range(CHUNKS):
        group = terms[c]
        for level in range(nbits - 1, 0, -1):
            half = len(group) // 2
            send = [t.astype(jnp.bfloat16) for t in group[half:]]
            *send, _ = lax.optimization_barrier((*send, last))
            group = [t + shifted(s, level).astype(jnp.float32) for t, s in zip(group[:half], send)]
        adjoint_modes.append((group[0] * weights).astype(jnp.bfloat16))
        send, _ = lax.optimization_barrier((parts[c][1].astype(jnp.bfloat16), last))
        total = parts[c][0] + shifted(send, 0).astype(jnp.float32)
        balancing.append((total * weights).astype(jnp.bfloat16))
    balancing = jnp.concatenate(balancing, 1).T
    adjoint_modes = jnp.concatenate(adjoint_modes, 1).T

    per_block = nrow_devices // nsnap
    width = block_cols // per_block
    pieces = swapped_by([tiles[e, a] for e in range(nsnap // 2) for a in range(2)], me)
    stacked = jnp.concatenate(
        [t[:, h * width : (h + 1) * width] for t in pieces for h in range(per_block)], 0
    )
    piece = lax.psum_scatter(stacked, "rows", scatter_dimension=0, tiled=True)
    piece = piece / jnp.sqrt(jnp.float32(nrows))
    route = []
    for r in range(nrow_devices):
        j = r // per_block
        target = (j ^ 1) * per_block + r % per_block
        for s in range(nsnap):
            if j % 2 != s % 2:
                route.append((r * nsnap + s, target * nsnap + (s ^ 1)))
    crossed = lax.ppermute(piece, ("rows", "snap"), route)
    gram = jnp.where((my_row // per_block) % 2 == me % 2, piece, crossed)
    return (gram, balancing, adjoint_modes)


def solution(mesh):
    return jax.shard_map(
        on_device,
        mesh=mesh,
        in_specs=(P("rows", "snap"), P("rows", "snap"), P(), P(), P()),
        out_specs=(P("snap", "rows"), P("rows", "snap"), P("rows", "snap")),
        check_vma=False,
    )
```

```python
import functools
import math

import jax
import jax.numpy as jnp
from jax import lax
from jax.experimental import pallas as pl
from jax.experimental.pallas import tpu as pltpu
from jax.sharding import PartitionSpec as P

MESH = pl.DeviceIdType.MESH
CHUNKS = 8


def flipped(index, mask, bits):
    total = 0
    for b in range(bits):
        bit = (index // (1 << b)) % 2
        total = total + (1 << b) * ((1 - bit) if (mask >> b) & 1 else bit)
    return total


def kernel(
    nsnap, nrow, nchunks, root,
    x_hbm, y_hbm, vt, ut, weights, gram, balancing, adjoint_modes,
    x_own, y_own, x_oth, y_oth,
    bal_own, adj_own, bal_send, bal_recv, adj_send, adj_recv,
    acc, stage, slots, piece, crossed,
    local_sem, x_s, x_r, y_s, y_r, bal_s, bal_r, adj_s, adj_r, rs_s, rs_r, cross_s, cross_r,
):
    bits = nsnap.bit_length() - 1
    couples = nsnap // 2
    rows = x_own.shape[1]
    mode_cols = bal_own.shape[1]
    per_block = nrow // nsnap
    width = piece.shape[1]
    me = lax.axis_index("snap")
    row = lax.axis_index("rows")
    partner = flipped(me, 1, bits)
    far = [flipped(me, 2 * e, bits) for e in range(1, couples)]
    block = row // per_block
    opposite = row + per_block * (1 - 2 * (block % 2))
    outer = (me + me // 2) % 2 == 0
    crossing = (block + me) % 2 == 1

    def remote(src, dst, send, recv, target):
        return pltpu.make_async_remote_copy(
            src_ref=src, dst_ref=dst, send_sem=send, recv_sem=recv,
            device_id=target, device_id_type=MESH,
        )

    def x_copy(e, c):
        return remote(
            x_hbm.at[pl.ds(c * rows, rows)], x_oth.at[e, c], x_s.at[e, c], x_r.at[e, c], (row, far[e])
        )

    def y_copy(c):
        return remote(
            y_hbm.at[pl.ds(c * rows, rows)], y_oth.at[c], y_s.at[c], y_r.at[c], (row, partner)
        )

    def bal_copy(c):
        return remote(bal_send.at[c], bal_recv.at[c], bal_s.at[c], bal_r.at[c], (row, partner))

    def adj_copy(e, c):
        return remote(
            adj_send.at[e, c], adj_recv.at[e, c], adj_s.at[e, c], adj_r.at[e, c], (row, far[e])
        )

    def rs_copy(d):
        target = (row + d) % nrow
        return remote(stage.at[target], slots.at[d - 1], rs_s.at[d - 1], rs_r.at[d - 1], (target, me))

    def x_local(c):
        return pltpu.make_async_copy(x_hbm.at[pl.ds(c * rows, rows)], x_own.at[c], local_sem.at[0, c])

    def y_local(c):
        return pltpu.make_async_copy(y_hbm.at[pl.ds(c * rows, rows)], y_own.at[c], local_sem.at[1, c])

    def each(body):
        def step(c, carry):
            body(c)
            return carry

        lax.fori_loop(0, nchunks, step, 0)

    def each_far(make, act):
        def body(c):
            for e in range(couples - 1):
                act(make(e, c))

        each(body)

    start = lambda copy: copy.start()
    sent = lambda copy: copy.wait_send()

    barrier = pltpu.get_barrier_semaphore()
    peers = [(row, partner), (opposite, partner)] + [(row, f) for f in far]
    peers += [((row + d) % nrow, me) for d in range(1, nrow)]
    for peer in peers:
        pl.semaphore_signal(barrier, inc=1, device_id=peer, device_id_type=MESH)
    pl.semaphore_wait(barrier, len(peers))

    @pl.when(outer)
    def _():
        each(lambda c: start(y_copy(c)))
        each_far(x_copy, start)

    @pl.when(jnp.logical_not(outer))
    def _():
        each_far(x_copy, start)

    each(lambda c: (start(x_local(c)), start(y_local(c))))
    acc[...] = jnp.zeros_like(acc)

    @pl.when(jnp.logical_not(outer))
    def _():
        each_far(x_copy, sent)
        each(lambda c: start(y_copy(c)))

    def consume(c):
        x_local(c).wait()
        y_local(c).wait()
        y_copy(c).wait_recv()
        for e in range(couples - 1):
            x_copy(e, c).wait_recv()
        ys = (y_own.at[c], y_oth.at[c])
        xs = [x_own.at[c]] + [x_oth.at[e, c] for e in range(couples - 1)]
        for e in range(couples):
            for a in range(2):
                acc[2 * e + a] += lax.dot_general(
                    ys[a][...], xs[e][...], (((0,), (0,)), ((), ())), preferred_element_type=jnp.float32
                )
        nt = (((1,), (1,)), ((), ()))
        part = sum(
            lax.dot_general(vt[e], xs[e][...], nt, preferred_element_type=jnp.float32)
            for e in range(couples)
        )
        bal_own[c] = part[:mode_cols]
        bal_send[c] = part[mode_cols:].astype(jnp.bfloat16)
        term = sum(
            lax.dot_general(ut[a], ys[a][...], nt, preferred_element_type=jnp.float32) for a in range(2)
        )
        adj_own[c] = term[:mode_cols]
        for e in range(1, couples):
            adj_send[e - 1, c] = term[e * mode_cols : (e + 1) * mode_cols].astype(jnp.bfloat16)

    each(consume)

    for k in range(nsnap):
        target = flipped(me, k, bits) * per_block
        for h in range(per_block):
            stage[target + h] = acc[k, :, h * width : (h + 1) * width]
    for d in range(1, nrow):
        rs_copy(d).start()

    @pl.when(outer)
    def _():
        each(lambda c: start(bal_copy(c)))

    @pl.when(jnp.logical_not(outer))
    def _():
        each_far(adj_copy, start)

    total = stage[row]
    for d in range(1, nrow):
        rs_copy(d).wait_recv()
        total = total + slots[d - 1]
    piece[...] = total / jnp.float32(root)
    cross = remote(piece, crossed, cross_s, cross_r, (opposite, partner))

    @pl.when(crossing)
    def _():
        cross.start()

    @pl.when(outer)
    def _():
        each_far(adj_copy, start)
        each(lambda c: sent(y_copy(c)))
        each_far(x_copy, sent)
        each(lambda c: sent(bal_copy(c)))

    @pl.when(jnp.logical_not(outer))
    def _():
        each(lambda c: sent(y_copy(c)))
        each_far(adj_copy, sent)
        each(lambda c: start(bal_copy(c)))

    scale = weights[...]

    def finish(c):
        bal_copy(c).wait_recv()
        span = pl.ds(pl.multiple_of(c * rows, rows), rows)
        balancing[:, span] = ((bal_own[c] + bal_recv[c].astype(jnp.float32)) * scale).astype(jnp.bfloat16)
        value = adj_own[c]
        for e in range(couples - 1):
            adj_copy(e, c).wait_recv()
            value = value + adj_recv[e, c].astype(jnp.float32)
        adjoint_modes[:, span] = (value * scale).astype(jnp.bfloat16)

    each(finish)

    @pl.when(crossing)
    def _():
        cross.wait()
        gram[...] = crossed[...]

    @pl.when(jnp.logical_not(crossing))
    def _():
        gram[...] = piece[...]

    @pl.when(outer)
    def _():
        each_far(adj_copy, sent)

    @pl.when(jnp.logical_not(outer))
    def _():
        each(lambda c: sent(bal_copy(c)))

    for d in range(1, nrow):
        rs_copy(d).wait_send()


def on_device(direct, adjoint, right_vectors, left_vectors, singular):
    local_rows, block_cols = direct.shape
    nsnap = lax.axis_size("snap")
    nrow = lax.axis_size("rows")
    couples = nsnap // 2
    mode_cols = right_vectors.shape[1] // nsnap
    me = lax.axis_index("snap")
    root = math.sqrt(local_rows * nrow)
    weights = lax.rsqrt(lax.dynamic_slice_in_dim(singular, me * mode_cols, mode_cols, 0))[:, None]

    def part(vectors, row_block, mode_block):
        return lax.dynamic_slice(
            vectors, (row_block * block_cols, mode_block * mode_cols), (block_cols, mode_cols)
        ).T

    vt = jnp.stack(
        [
            jnp.concatenate([part(right_vectors, me ^ (2 * e), me ^ a) for a in range(2)], 0)
            for e in range(couples)
        ]
    )
    ut = jnp.stack(
        [
            jnp.concatenate([part(left_vectors, me ^ a, me ^ (2 * e)) for e in range(couples)], 0)
            for a in range(2)
        ]
    )
    nchunks = CHUNKS
    rows = local_rows // nchunks
    width = block_cols * nsnap // nrow
    vmem = pl.BlockSpec(memory_space=pltpu.VMEM)
    hbm = pl.BlockSpec(memory_space=pl.ANY)
    bf16, f32, dma = jnp.bfloat16, jnp.float32, pltpu.SemaphoreType.DMA
    modes = (nchunks, mode_cols, rows)
    gram, balancing, adjoint_modes = pl.pallas_call(
        functools.partial(kernel, nsnap, nrow, nchunks, root),
        out_shape=(
            jax.ShapeDtypeStruct((block_cols, width), f32),
            jax.ShapeDtypeStruct((mode_cols, local_rows), bf16),
            jax.ShapeDtypeStruct((mode_cols, local_rows), bf16),
        ),
        in_specs=[hbm, hbm, vmem, vmem, vmem],
        out_specs=(vmem, vmem, vmem),
        scratch_shapes=[
            pltpu.VMEM((nchunks, rows, block_cols), bf16),
            pltpu.VMEM((nchunks, rows, block_cols), bf16),
            pltpu.VMEM((couples - 1, nchunks, rows, block_cols), bf16),
            pltpu.VMEM((nchunks, rows, block_cols), bf16),
            pltpu.VMEM(modes, f32),
            pltpu.VMEM(modes, f32),
            pltpu.VMEM(modes, bf16),
            pltpu.VMEM(modes, bf16),
            pltpu.VMEM((couples - 1,) + modes, bf16),
            pltpu.VMEM((couples - 1,) + modes, bf16),
            pltpu.VMEM((nsnap, block_cols, block_cols), f32),
            pltpu.VMEM((nrow, block_cols, width), f32),
            pltpu.VMEM((nrow - 1, block_cols, width), f32),
            pltpu.VMEM((block_cols, width), f32),
            pltpu.VMEM((block_cols, width), f32),
            dma((2, nchunks)),
            dma((couples - 1, nchunks)),
            dma((couples - 1, nchunks)),
            dma((nchunks,)),
            dma((nchunks,)),
            dma((nchunks,)),
            dma((nchunks,)),
            dma((couples - 1, nchunks)),
            dma((couples - 1, nchunks)),
            dma((nrow - 1,)),
            dma((nrow - 1,)),
            dma(()),
            dma(()),
        ],
        compiler_params=pltpu.CompilerParams(
            collective_id=0, has_side_effects=True, vmem_limit_bytes=60 * 1024 * 1024
        ),
    )(direct, adjoint, vt, ut, weights)

    return (gram, balancing.T, adjoint_modes.T)


def solution(mesh):
    return jax.shard_map(
        on_device,
        mesh=mesh,
        in_specs=(P("rows", "snap"), P("rows", "snap"), P(), P(), P()),
        out_specs=(P("snap", "rows"), P("rows", "snap"), P("rows", "snap")),
        check_vma=False,
    )
```

```python
import functools
import math

import jax
import jax.numpy as jnp
from jax import lax
from jax.experimental import pallas as pl
from jax.experimental.pallas import tpu as pltpu
from jax.sharding import PartitionSpec as P

MESH = pl.DeviceIdType.MESH
CHUNKS = 8


def flipped(index, mask, bits):
    total = 0
    for b in range(bits):
        bit = (index // (1 << b)) % 2
        total = total + (1 << b) * ((1 - bit) if (mask >> b) & 1 else bit)
    return total


def kernel(
    nsnap, nrow, nchunks, root,
    x_hbm, y_hbm, vt, ut, weights, gram, balancing, adjoint_modes,
    x_own, y_own, x_oth, y_oth,
    bal_own, adj_own, bal_send, bal_recv, adj_send, adj_recv,
    acc, stage, slots, piece, crossed,
    local_sem, x_s, x_r, y_s, y_r, bal_s, bal_r, adj_s, adj_r, rs_s, rs_r, cross_s, cross_r,
):
    bits = nsnap.bit_length() - 1
    couples = nsnap // 2
    rows = x_own.shape[1]
    mode_cols = bal_own.shape[1]
    per_block = nrow // nsnap
    width = piece.shape[1]
    me = lax.axis_index("snap")
    row = lax.axis_index("rows")
    partner = flipped(me, 1, bits)
    far = [flipped(me, 2 * e, bits) for e in range(1, couples)]
    block = row // per_block
    opposite = row + per_block * (1 - 2 * (block % 2))
    outer = (me + me // 2) % 2 == 0
    crossing = (block + me) % 2 == 1

    def remote(src, dst, send, recv, target):
        return pltpu.make_async_remote_copy(
            src_ref=src, dst_ref=dst, send_sem=send, recv_sem=recv,
            device_id=target, device_id_type=MESH,
        )

    def x_copy(e, c):
        return remote(
            x_hbm.at[pl.ds(c * rows, rows)], x_oth.at[e, c], x_s.at[e, c], x_r.at[e, c], (row, far[e])
        )

    def y_copy(c):
        return remote(
            y_hbm.at[pl.ds(c * rows, rows)], y_oth.at[c], y_s.at[c], y_r.at[c], (row, partner)
        )

    def bal_copy(c):
        return remote(bal_send.at[c], bal_recv.at[c], bal_s.at[c], bal_r.at[c], (row, partner))

    def adj_copy(e, c):
        return remote(
            adj_send.at[e, c], adj_recv.at[e, c], adj_s.at[e, c], adj_r.at[e, c], (row, far[e])
        )

    def rs_copy(d):
        target = (row + d) % nrow
        return remote(stage.at[target], slots.at[d - 1], rs_s.at[d - 1], rs_r.at[d - 1], (target, me))

    def x_local(c):
        return pltpu.make_async_copy(x_hbm.at[pl.ds(c * rows, rows)], x_own.at[c], local_sem.at[0, c])

    def y_local(c):
        return pltpu.make_async_copy(y_hbm.at[pl.ds(c * rows, rows)], y_own.at[c], local_sem.at[1, c])

    def each(body):
        def step(c, carry):
            body(c)
            return carry

        lax.fori_loop(0, nchunks, step, 0)

    def each_far(make, act):
        def body(c):
            for e in range(couples - 1):
                act(make(e, c))

        each(body)

    start = lambda copy: copy.start()
    sent = lambda copy: copy.wait_send()

    barrier = pltpu.get_barrier_semaphore()
    peers = [(row, partner), (opposite, partner)] + [(row, f) for f in far]
    peers += [((row + d) % nrow, me) for d in range(1, nrow)]
    for peer in peers:
        pl.semaphore_signal(barrier, inc=1, device_id=peer, device_id_type=MESH)
    pl.semaphore_wait(barrier, len(peers))

    ys = lambda c: (y_own.at[c], y_oth.at[c])
    xs = lambda c: [x_own.at[c]] + [x_oth.at[e, c] for e in range(couples - 1)]
    nt = (((1,), (1,)), ((), ()))

    def bal_part(c):
        part = sum(
            lax.dot_general(vt[e], x[...], nt, preferred_element_type=jnp.float32)
            for e, x in enumerate(xs(c))
        )
        bal_own[c] = part[:mode_cols]
        bal_send[c] = part[mode_cols:].astype(jnp.bfloat16)

    def adj_part(c):
        term = sum(
            lax.dot_general(ut[a], y[...], nt, preferred_element_type=jnp.float32)
            for a, y in enumerate(ys(c))
        )
        adj_own[c] = term[:mode_cols]
        for e in range(1, couples):
            adj_send[e - 1, c] = term[e * mode_cols : (e + 1) * mode_cols].astype(jnp.bfloat16)

    def gram_part(c):
        for e, x in enumerate(xs(c)):
            for a, y in enumerate(ys(c)):
                acc[2 * e + a] += lax.dot_general(
                    y[...], x[...], (((0,), (0,)), ((), ())), preferred_element_type=jnp.float32
                )

    def x_arrived(c):
        x_local(c).wait()
        for e in range(couples - 1):
            x_copy(e, c).wait_recv()

    def y_arrived(c):
        y_local(c).wait()
        y_copy(c).wait_recv()

    def all_at_once():
        each(lambda c: start(y_copy(c)))
        each_far(x_copy, start)
        each(lambda c: (start(x_local(c)), start(y_local(c))))
        acc[...] = jnp.zeros_like(acc)

        def body(c):
            x_arrived(c)
            y_arrived(c)
            bal_part(c)
            bal_copy(c).start()
            adj_part(c)
            for e in range(couples - 1):
                adj_copy(e, c).start()
            gram_part(c)

        each(body)
        each_far(x_copy, sent)
        each_far(adj_copy, sent)

    def in_turns():
        @pl.when(outer)
        def _():
            each(lambda c: start(y_copy(c)))

        @pl.when(jnp.logical_not(outer))
        def _():
            each_far(x_copy, start)

        each(lambda c: (start(x_local(c)), start(y_local(c))))
        acc[...] = jnp.zeros_like(acc)

        @pl.when(outer)
        def _():
            def body(c):
                x_arrived(c)
                bal_part(c)
                bal_copy(c).start()

            each(body)
            each_far(x_copy, start)

            def later(c):
                y_arrived(c)
                adj_part(c)
                for e in range(couples - 1):
                    adj_copy(e, c).start()
                gram_part(c)

            each(later)

        @pl.when(jnp.logical_not(outer))
        def _():
            def body(c):
                y_arrived(c)
                adj_part(c)
                for e in range(couples - 1):
                    adj_copy(e, c).start()

            each(body)
            each_far(x_copy, sent)
            each_far(adj_copy, sent)
            each(lambda c: start(y_copy(c)))

            def later(c):
                x_arrived(c)
                bal_part(c)
                bal_copy(c).start()
                gram_part(c)

            each(later)

    if couples == 2:
        in_turns()
    else:
        all_at_once()

    for k in range(nsnap):
        target = flipped(me, k, bits) * per_block
        for h in range(per_block):
            stage[target + h] = acc[k, :, h * width : (h + 1) * width]
    for d in range(1, nrow):
        rs_copy(d).start()

    total = stage[row]
    for d in range(1, nrow):
        rs_copy(d).wait_recv()
        total = total + slots[d - 1]
    piece[...] = total / jnp.float32(root)
    cross = remote(piece, crossed, cross_s, cross_r, (opposite, partner))

    @pl.when(crossing)
    def _():
        cross.start()

    scale = weights[...]

    def finish(c):
        bal_copy(c).wait_recv()
        span = pl.ds(pl.multiple_of(c * rows, rows), rows)
        balancing[:, span] = ((bal_own[c] + bal_recv[c].astype(jnp.float32)) * scale).astype(jnp.bfloat16)
        value = adj_own[c]
        for e in range(couples - 1):
            adj_copy(e, c).wait_recv()
            value = value + adj_recv[e, c].astype(jnp.float32)
        adjoint_modes[:, span] = (value * scale).astype(jnp.bfloat16)

    each(finish)

    @pl.when(crossing)
    def _():
        cross.wait()
        gram[...] = crossed[...]

    @pl.when(jnp.logical_not(crossing))
    def _():
        gram[...] = piece[...]

    each(lambda c: sent(y_copy(c)))
    each(lambda c: sent(bal_copy(c)))

    if couples == 2:

        @pl.when(outer)
        def _():
            each_far(x_copy, sent)
            each_far(adj_copy, sent)

    for d in range(1, nrow):
        rs_copy(d).wait_send()


def on_device(direct, adjoint, right_vectors, left_vectors, singular):
    local_rows, block_cols = direct.shape
    nsnap = lax.axis_size("snap")
    nrow = lax.axis_size("rows")
    couples = nsnap // 2
    mode_cols = right_vectors.shape[1] // nsnap
    me = lax.axis_index("snap")
    root = math.sqrt(local_rows * nrow)
    weights = lax.rsqrt(lax.dynamic_slice_in_dim(singular, me * mode_cols, mode_cols, 0))[:, None]

    def part(vectors, row_block, mode_block):
        return lax.dynamic_slice(
            vectors, (row_block * block_cols, mode_block * mode_cols), (block_cols, mode_cols)
        ).T

    vt = jnp.stack(
        [
            jnp.concatenate([part(right_vectors, me ^ (2 * e), me ^ a) for a in range(2)], 0)
            for e in range(couples)
        ]
    )
    ut = jnp.stack(
        [
            jnp.concatenate([part(left_vectors, me ^ a, me ^ (2 * e)) for e in range(couples)], 0)
            for a in range(2)
        ]
    )
    nchunks = CHUNKS
    rows = local_rows // nchunks
    width = block_cols * nsnap // nrow
    vmem = pl.BlockSpec(memory_space=pltpu.VMEM)
    hbm = pl.BlockSpec(memory_space=pl.ANY)
    bf16, f32, dma = jnp.bfloat16, jnp.float32, pltpu.SemaphoreType.DMA
    modes = (nchunks, mode_cols, rows)
    gram, balancing, adjoint_modes = pl.pallas_call(
        functools.partial(kernel, nsnap, nrow, nchunks, root),
        out_shape=(
            jax.ShapeDtypeStruct((block_cols, width), f32),
            jax.ShapeDtypeStruct((mode_cols, local_rows), bf16),
            jax.ShapeDtypeStruct((mode_cols, local_rows), bf16),
        ),
        in_specs=[hbm, hbm, vmem, vmem, vmem],
        out_specs=(vmem, vmem, vmem),
        scratch_shapes=[
            pltpu.VMEM((nchunks, rows, block_cols), bf16),
            pltpu.VMEM((nchunks, rows, block_cols), bf16),
            pltpu.VMEM((couples - 1, nchunks, rows, block_cols), bf16),
            pltpu.VMEM((nchunks, rows, block_cols), bf16),
            pltpu.VMEM(modes, f32),
            pltpu.VMEM(modes, f32),
            pltpu.VMEM(modes, bf16),
            pltpu.VMEM(modes, bf16),
            pltpu.VMEM((couples - 1,) + modes, bf16),
            pltpu.VMEM((couples - 1,) + modes, bf16),
            pltpu.VMEM((nsnap, block_cols, block_cols), f32),
            pltpu.VMEM((nrow, block_cols, width), f32),
            pltpu.VMEM((nrow - 1, block_cols, width), f32),
            pltpu.VMEM((block_cols, width), f32),
            pltpu.VMEM((block_cols, width), f32),
            dma((2, nchunks)),
            dma((couples - 1, nchunks)),
            dma((couples - 1, nchunks)),
            dma((nchunks,)),
            dma((nchunks,)),
            dma((nchunks,)),
            dma((nchunks,)),
            dma((couples - 1, nchunks)),
            dma((couples - 1, nchunks)),
            dma((nrow - 1,)),
            dma((nrow - 1,)),
            dma(()),
            dma(()),
        ],
        compiler_params=pltpu.CompilerParams(
            collective_id=0, has_side_effects=True, vmem_limit_bytes=60 * 1024 * 1024
        ),
    )(direct, adjoint, vt, ut, weights)

    return (gram, balancing.T, adjoint_modes.T)


def solution(mesh):
    return jax.shard_map(
        on_device,
        mesh=mesh,
        in_specs=(P("rows", "snap"), P("rows", "snap"), P(), P(), P()),
        out_specs=(P("snap", "rows"), P("rows", "snap"), P("rows", "snap")),
        check_vma=False,
    )
```

```python
import functools
import math

import jax
import jax.numpy as jnp
from jax import lax
from jax.experimental import pallas as pl
from jax.experimental.pallas import tpu as pltpu
from jax.sharding import PartitionSpec as P

MESH = pl.DeviceIdType.MESH
CHUNKS = 8


def flipped(index, mask, bits):
    total = 0
    for b in range(bits):
        bit = (index // (1 << b)) % 2
        total = total + (1 << b) * ((1 - bit) if (mask >> b) & 1 else bit)
    return total


def kernel(
    nsnap, nrow, nchunks, root,
    x_hbm, y_hbm, vt, ut, weights, gram, balancing, adjoint_modes,
    x_own, y_own, x_oth, y_oth,
    bal_own, adj_own, bal_send, bal_recv, adj_send, adj_recv,
    acc, stage, slots, piece, crossed,
    local_sem, x_s, x_r, y_s, y_r, bal_s, bal_r, adj_s, adj_r, rs_s, rs_r, cross_s, cross_r,
):
    bits = nsnap.bit_length() - 1
    couples = nsnap // 2
    rows = x_own.shape[1]
    mode_cols = bal_own.shape[1]
    per_block = nrow // nsnap
    width = piece.shape[1]
    me = lax.axis_index("snap")
    row = lax.axis_index("rows")
    partner = flipped(me, 1, bits)
    far = [flipped(me, 2 * e, bits) for e in range(1, couples)]
    block = row // per_block
    opposite = row + per_block * (1 - 2 * (block % 2))
    outer = (me + me // 2) % 2 == 0
    crossing = (block + me) % 2 == 1

    def remote(src, dst, send, recv, target):
        return pltpu.make_async_remote_copy(
            src_ref=src, dst_ref=dst, send_sem=send, recv_sem=recv,
            device_id=target, device_id_type=MESH,
        )

    def x_copy(e, c):
        return remote(
            x_hbm.at[pl.ds(c * rows, rows)], x_oth.at[e, c], x_s.at[e, c], x_r.at[e, c], (row, far[e])
        )

    def y_copy(c):
        return remote(
            y_hbm.at[pl.ds(c * rows, rows)], y_oth.at[c], y_s.at[c], y_r.at[c], (row, partner)
        )

    def bal_copy(c):
        return remote(bal_send.at[c], bal_recv.at[c], bal_s.at[c], bal_r.at[c], (row, partner))

    def adj_copy(e, c):
        return remote(
            adj_send.at[e, c], adj_recv.at[e, c], adj_s.at[e, c], adj_r.at[e, c], (row, far[e])
        )

    def rs_copy(d):
        target = (row + d) % nrow
        return remote(stage.at[target], slots.at[d - 1], rs_s.at[d - 1], rs_r.at[d - 1], (target, me))

    def x_local(c):
        return pltpu.make_async_copy(x_hbm.at[pl.ds(c * rows, rows)], x_own.at[c], local_sem.at[0, c])

    def y_local(c):
        return pltpu.make_async_copy(y_hbm.at[pl.ds(c * rows, rows)], y_own.at[c], local_sem.at[1, c])

    def each(body):
        def step(c, carry):
            body(c)
            return carry

        lax.fori_loop(0, nchunks, step, 0)

    def each_far(make, act):
        def body(c):
            for e in range(couples - 1):
                act(make(e, c))

        each(body)

    start = lambda copy: copy.start()
    sent = lambda copy: copy.wait_send()

    barrier = pltpu.get_barrier_semaphore()
    peers = [(row, partner), (opposite, partner)] + [(row, f) for f in far]
    peers += [((row + d) % nrow, me) for d in range(1, nrow)]
    for peer in peers:
        pl.semaphore_signal(barrier, inc=1, device_id=peer, device_id_type=MESH)
    pl.semaphore_wait(barrier, len(peers))

    ys = lambda c: (y_own.at[c], y_oth.at[c])
    xs = lambda c: [x_own.at[c]] + [x_oth.at[e, c] for e in range(couples - 1)]
    nt = (((1,), (1,)), ((), ()))

    def bal_part(c):
        part = sum(
            lax.dot_general(vt[e], x[...], nt, preferred_element_type=jnp.float32)
            for e, x in enumerate(xs(c))
        )
        bal_own[c] = part[:mode_cols]
        bal_send[c] = part[mode_cols:].astype(jnp.bfloat16)

    def adj_part(c):
        term = sum(
            lax.dot_general(ut[a], y[...], nt, preferred_element_type=jnp.float32)
            for a, y in enumerate(ys(c))
        )
        adj_own[c] = term[:mode_cols]
        for e in range(1, couples):
            adj_send[e - 1, c] = term[e * mode_cols : (e + 1) * mode_cols].astype(jnp.bfloat16)

    def gram_part(c):
        for e, x in enumerate(xs(c)):
            for a, y in enumerate(ys(c)):
                acc[2 * e + a] += lax.dot_general(
                    y[...], x[...], (((0,), (0,)), ((), ())), preferred_element_type=jnp.float32
                )

    def x_arrived(c):
        x_local(c).wait()
        for e in range(couples - 1):
            x_copy(e, c).wait_recv()

    def y_arrived(c):
        y_local(c).wait()
        y_copy(c).wait_recv()

    def all_at_once():
        each(lambda c: start(y_copy(c)))
        each_far(x_copy, start)
        each(lambda c: (start(x_local(c)), start(y_local(c))))
        acc[...] = jnp.zeros_like(acc)

        def body(c):
            x_arrived(c)
            y_arrived(c)
            bal_part(c)
            bal_copy(c).start()
            adj_part(c)
            for e in range(couples - 1):
                adj_copy(e, c).start()
            gram_part(c)

        each(body)
        each_far(x_copy, sent)
        each_far(adj_copy, sent)

    def in_turns():
        @pl.when(outer)
        def _():
            each(lambda c: start(y_copy(c)))

        @pl.when(jnp.logical_not(outer))
        def _():
            each_far(x_copy, start)

        each(lambda c: (start(x_local(c)), start(y_local(c))))
        acc[...] = jnp.zeros_like(acc)

        @pl.when(outer)
        def _():
            def body(c):
                x_arrived(c)
                bal_part(c)
                bal_copy(c).start()

            each(body)
            each_far(x_copy, start)

            def later(c):
                y_arrived(c)
                adj_part(c)
                for e in range(couples - 1):
                    adj_copy(e, c).start()
                gram_part(c)

            each(later)

        @pl.when(jnp.logical_not(outer))
        def _():
            def body(c):
                y_arrived(c)
                adj_part(c)
                for e in range(couples - 1):
                    adj_copy(e, c).start()

            each(body)
            each_far(x_copy, sent)
            each_far(adj_copy, sent)
            each(lambda c: start(y_copy(c)))

            def later(c):
                x_arrived(c)
                bal_part(c)
                bal_copy(c).start()
                gram_part(c)

            each(later)

    if couples == 2:
        in_turns()
    else:
        all_at_once()

    for k in range(nsnap):
        target = flipped(me, k, bits) * per_block
        for h in range(per_block):
            stage[target + h] = acc[k, :, h * width : (h + 1) * width]
    for d in range(1, nrow):
        rs_copy(d).start()

    total = stage[row]
    for d in range(1, nrow):
        rs_copy(d).wait_recv()
        total = total + slots[d - 1]
    piece[...] = total / jnp.float32(root)
    cross = remote(piece, crossed, cross_s, cross_r, (opposite, partner))

    @pl.when(crossing)
    def _():
        cross.start()

    scale = weights[...]

    def finish(c):
        bal_copy(c).wait_recv()
        span = pl.ds(pl.multiple_of(c * rows, rows), rows)
        balancing[:, span] = ((bal_own[c] + bal_recv[c].astype(jnp.float32)) * scale).astype(jnp.bfloat16)
        value = adj_own[c]
        for e in range(couples - 1):
            adj_copy(e, c).wait_recv()
            value = value + adj_recv[e, c].astype(jnp.float32)
        adjoint_modes[:, span] = (value * scale).astype(jnp.bfloat16)

    each(finish)

    @pl.when(crossing)
    def _():
        cross.wait()
        gram[...] = crossed[...]

    @pl.when(jnp.logical_not(crossing))
    def _():
        gram[...] = piece[...]

    each(lambda c: sent(y_copy(c)))
    each(lambda c: sent(bal_copy(c)))

    if couples == 2:

        @pl.when(outer)
        def _():
            each_far(x_copy, sent)
            each_far(adj_copy, sent)

    for d in range(1, nrow):
        rs_copy(d).wait_send()


def on_device(direct, adjoint, right_vectors, left_vectors, singular):
    local_rows, block_cols = direct.shape
    nsnap = lax.axis_size("snap")
    nrow = lax.axis_size("rows")
    couples = nsnap // 2
    mode_cols = right_vectors.shape[1] // nsnap
    me = lax.axis_index("snap")
    root = math.sqrt(local_rows * nrow)
    weights = lax.rsqrt(lax.dynamic_slice_in_dim(singular, me * mode_cols, mode_cols, 0))[:, None]

    def part(vectors, row_block, mode_block):
        return lax.dynamic_slice(
            vectors, (row_block * block_cols, mode_block * mode_cols), (block_cols, mode_cols)
        ).T

    vt = jnp.stack(
        [
            jnp.concatenate([part(right_vectors, me ^ (2 * e), me ^ a) for a in range(2)], 0)
            for e in range(couples)
        ]
    )
    ut = jnp.stack(
        [
            jnp.concatenate([part(left_vectors, me ^ a, me ^ (2 * e)) for e in range(couples)], 0)
            for a in range(2)
        ]
    )
    nchunks = CHUNKS
    rows = local_rows // nchunks
    width = block_cols * nsnap // nrow
    vmem = pl.BlockSpec(memory_space=pltpu.VMEM)
    hbm = pl.BlockSpec(memory_space=pl.ANY)
    bf16, f32, dma = jnp.bfloat16, jnp.float32, pltpu.SemaphoreType.DMA
    modes = (nchunks, mode_cols, rows)
    gram, balancing, adjoint_modes = pl.pallas_call(
        functools.partial(kernel, nsnap, nrow, nchunks, root),
        out_shape=(
            jax.ShapeDtypeStruct((block_cols, width), f32),
            jax.ShapeDtypeStruct((mode_cols, local_rows), bf16),
            jax.ShapeDtypeStruct((mode_cols, local_rows), bf16),
        ),
        in_specs=[hbm, hbm, vmem, vmem, vmem],
        out_specs=(vmem, vmem, vmem),
        scratch_shapes=[
            pltpu.VMEM((nchunks, rows, block_cols), bf16),
            pltpu.VMEM((nchunks, rows, block_cols), bf16),
            pltpu.VMEM((couples - 1, nchunks, rows, block_cols), bf16),
            pltpu.VMEM((nchunks, rows, block_cols), bf16),
            pltpu.VMEM(modes, f32),
            pltpu.VMEM(modes, f32),
            pltpu.VMEM(modes, bf16),
            pltpu.VMEM(modes, bf16),
            pltpu.VMEM((couples - 1,) + modes, bf16),
            pltpu.VMEM((couples - 1,) + modes, bf16),
            pltpu.VMEM((nsnap, block_cols, block_cols), f32),
            pltpu.VMEM((nrow, block_cols, width), f32),
            pltpu.VMEM((nrow - 1, block_cols, width), f32),
            pltpu.VMEM((block_cols, width), f32),
            pltpu.VMEM((block_cols, width), f32),
            dma((2, nchunks)),
            dma((couples - 1, nchunks)),
            dma((couples - 1, nchunks)),
            dma((nchunks,)),
            dma((nchunks,)),
            dma((nchunks,)),
            dma((nchunks,)),
            dma((couples - 1, nchunks)),
            dma((couples - 1, nchunks)),
            dma((nrow - 1,)),
            dma((nrow - 1,)),
            dma(()),
            dma(()),
        ],
        compiler_params=pltpu.CompilerParams(
            collective_id=0, has_side_effects=True, vmem_limit_bytes=36 * 1024 * 1024
        ),
    )(direct, adjoint, vt, ut, weights)

    return (gram, balancing.T, adjoint_modes.T)


def solution(mesh):
    return jax.shard_map(
        on_device,
        mesh=mesh,
        in_specs=(P("rows", "snap"), P("rows", "snap"), P(), P(), P()),
        out_specs=(P("snap", "rows"), P("rows", "snap"), P("rows", "snap")),
        check_vma=False,
    )
```
